512 devices in a mesh: tm: 32 (over x, z_lo), height: 8 (over z_hi, y), dp: 2 (over core).
Axes of the slice: x: 4, y: 4, z: 16 (z_hi: 2, z_lo: 8; z = z_hi * 8 + z_lo), core: 2. Of those that a mesh axis runs over, the one named last changes fastest.
Arguments:
- frames_in: bfloat16 [2, 128, 32, 48, 256], P('dp', 'tm', 'height'), may hold values from -6 to 6
- cotangent: bfloat16 [2, 128, 32, 48, 256], P('dp', 'tm', 'height'), may hold values from -6 to 6
- w_spatial: bfloat16 [3, 3, 256, 256], replicated, may hold values from -0.125 to 0.125
- w_temporal: bfloat16 [3, 256, 256], replicated, may hold values from -0.21875 to 0.21875
Outputs:
- decoded: bfloat16 [2, 128, 32, 48, 256], P('dp', 'tm', 'height')
- input_grad: bfloat16 [2, 128, 32, 48, 256], P('dp', 'tm', 'height')
- spatial_grad: bfloat16 [3, 3, 256, 256], replicated
- temporal_grad: bfloat16 [3, 256, 256], replicated
The draws below stay inside these ranges and needn't reach their ends.
All inputs are finite; a program needn't handle non-finite values.
Results may differ from the reference program's by a relative error of at most 0.0061.
Values may be sent and summed in bfloat16 or wider, within the bound.
No kernel may reach another device: no remote copies, remote signals or barrier semaphores. Data moves between devices by JAX's collectives and lax.ppermute only.
A program may use at most 64 MiB of HBM per device.

```python
import math
import jax
import jax.numpy as jnp
from jax import lax

CH = 256
COLS = 48
FRAMES = 128
ROWS = 32
CELLS = 393216
N_DP = 2


def levels(key, shape, cuts, least, top_value):
    def one(axis_at, shards_of):
        heights = jax.random.uniform(jax.random.fold_in(jax.random.fold_in(key, 6), axis_at), (shards_of,), jnp.float32, least / len(cuts), top_value / len(cuts))
        return jnp.repeat(jnp.exp(heights), shape[axis_at] // shards_of).reshape((-1,) + (1,) * (len(shape) - axis_at - 1))

    level = one(*cuts[0])
    for cut in cuts[1:]:
        level = level * one(*cut)
    return level


def bell_draw(rng, dims, scale, most, cuts=(), kind=jnp.bfloat16):
    drawn = jax.random.normal(rng, dims, jnp.float32) * scale
    if len(cuts) > 0:
        drawn = levels(rng, dims, cuts, -0.22, 0.18) * drawn
    return jnp.clip(drawn, min=-most, max=most).astype(kind)


def setup_inputs(seed: int = 0) -> dict:
    arg_keys = jax.random.split(jax.random.key(seed), 5)
    return {
        "frames_in": bell_draw(arg_keys[0], (N_DP, FRAMES, ROWS, COLS, CH), 1.0, 6.0, ((0, 2), (1, 32), (2, 8))),
        "cotangent": bell_draw(arg_keys[1], (N_DP, FRAMES, ROWS, COLS, CH), 1.0, 6.0, ((0, 2), (1, 32), (2, 8))),
        "w_spatial": bell_draw(arg_keys[2], (3, 3, CH, CH), (9 * CH) ** -0.5, 0.125),
        "w_temporal": bell_draw(arg_keys[3], (3, CH, CH), (3 * CH) ** -0.5, 0.21875),
    }


def silu_slope(values):
    sigmoid_value = jax.nn.sigmoid(values)
    return sigmoid_value * (1.0 + values * (1.0 - sigmoid_value))

def forward_taps(padded, row_count, col_count):
    pieces = [padded[row_tap:row_tap + row_count, col_tap:col_tap + col_count] for row_tap in range(3) for col_tap in range(3)]
    return jnp.concatenate(pieces, axis=-1)

def backward_taps(padded, row_count, col_count):
    pieces = [padded[2 - row_tap:2 - row_tap + row_count, 2 - col_tap:2 - col_tap + col_count] for row_tap in range(3) for col_tap in range(3)]
    return jnp.concatenate(pieces, axis=-1)

def reference(frames_in, cotangent, w_spatial, w_temporal):
    channels = w_temporal.shape[-1]
    spatial_flat = w_spatial.reshape(9 * channels, channels)
    temporal_flat = w_temporal.reshape(3 * channels, channels)
    spatial_back = jnp.concatenate([w_spatial[row_tap, col_tap].T for row_tap in range(3) for col_tap in range(3)], axis=0)
    temporal_back = jnp.concatenate([w_temporal[2].T, w_temporal[1].T, w_temporal[0].T], axis=0)
    contract = (((0,), (0,)), ((), ()))

    def one_clip(operands):
        inputs, upstream = operands
        activated = jax.nn.silu(inputs.astype(jnp.float32)).astype(jnp.bfloat16)

        def spatial_frame(frame):
            padded = jnp.pad(frame, ((1, 1), (1, 1), (0, 0)))
            stacked = forward_taps(padded, ROWS, COLS).reshape(-1, 9 * channels)
            product = jnp.dot(stacked, spatial_flat, preferred_element_type=jnp.float32)
            return product.astype(jnp.bfloat16).reshape(ROWS, COLS, channels)
        spatial_out = lax.map(spatial_frame, activated)
        padded_frames = jnp.concatenate([spatial_out[:1], spatial_out[:1], spatial_out], axis=0)
        upstream_ext = jnp.concatenate([upstream, jnp.zeros((2, ROWS, COLS, channels), jnp.bfloat16)], axis=0)

        def temporal_frame(index):
            slab = lax.dynamic_slice_in_dim(padded_frames, index, 3, 0)
            stacked = jnp.concatenate([slab[0], slab[1], slab[2]], axis=-1).reshape(-1, 3 * channels)
            grad_slab = lax.dynamic_slice_in_dim(upstream_ext, index, 3, 0)
            grad_stack = jnp.concatenate([grad_slab[0], grad_slab[1], grad_slab[2]], axis=-1).reshape(-1, 3 * channels)
            forward_part = jnp.dot(stacked, temporal_flat, preferred_element_type=jnp.float32)
            backward_part = jnp.dot(grad_stack, temporal_back, preferred_element_type=jnp.float32)
            return (forward_part.reshape(ROWS, COLS, channels), backward_part.reshape(ROWS, COLS, channels))
        frame_index = jnp.arange(FRAMES, dtype=jnp.int32)
        temporal_out, frame_sum = lax.map(temporal_frame, frame_index)
        first_up = upstream[0].reshape(-1, channels)
        second_up = upstream[1].reshape(-1, channels)
        fold_term = jnp.dot(first_up, w_temporal[0].T, preferred_element_type=jnp.float32)
        fold_term = fold_term + jnp.dot(first_up, w_temporal[1].T, preferred_element_type=jnp.float32)
        fold_term = fold_term + jnp.dot(second_up, w_temporal[0].T, preferred_element_type=jnp.float32)
        frame_sum = frame_sum.at[0].add(fold_term.reshape(ROWS, COLS, channels))
        frame_grad = frame_sum.astype(jnp.bfloat16)
        decoded = (inputs.astype(jnp.float32) + temporal_out).astype(jnp.bfloat16)

        def back_frame(frame):
            padded = jnp.pad(frame, ((1, 1), (1, 1), (0, 0)))
            stacked = backward_taps(padded, ROWS, COLS).reshape(-1, 9 * channels)
            return jnp.dot(stacked, spatial_back, preferred_element_type=jnp.float32).reshape(ROWS, COLS, channels)
        act_grad = lax.map(back_frame, frame_grad)
        input_grad = (upstream.astype(jnp.float32) + silu_slope(inputs.astype(jnp.float32)) * act_grad).astype(jnp.bfloat16)

        def accumulate(carry, index):
            spatial_acc, temporal_acc = carry
            frame = lax.dynamic_index_in_dim(activated, index, 0, keepdims=False)
            padded = jnp.pad(frame, ((1, 1), (1, 1), (0, 0)))
            stacked = forward_taps(padded, ROWS, COLS).reshape(-1, 9 * channels)
            grad_frame = lax.dynamic_index_in_dim(frame_grad, index, 0, keepdims=False).reshape(-1, channels)
            spatial_acc = spatial_acc + lax.dot_general(stacked, grad_frame, contract, preferred_element_type=jnp.float32)
            slab = lax.dynamic_slice_in_dim(padded_frames, index, 3, 0)
            frame_stack = jnp.concatenate([slab[0], slab[1], slab[2]], axis=-1).reshape(-1, 3 * channels)
            up_frame = lax.dynamic_index_in_dim(upstream, index, 0, keepdims=False).reshape(-1, channels)
            temporal_acc = temporal_acc + lax.dot_general(frame_stack, up_frame, contract, preferred_element_type=jnp.float32)
            return ((spatial_acc, temporal_acc), None)
        start = (jnp.zeros((9 * channels, channels), jnp.float32), jnp.zeros((3 * channels, channels), jnp.float32))
        (spatial_acc, temporal_acc), unused = lax.scan(accumulate, start, frame_index)
        return (decoded, input_grad, spatial_acc, temporal_acc)
    decoded, input_grad, spatial_sums, temporal_sums = lax.map(one_clip, (frames_in, cotangent))
    grad_scale = 1.0 / math.sqrt(CELLS)
    spatial_grad = (lax.optimization_barrier(jnp.sum(spatial_sums, axis=0)) * grad_scale).astype(jnp.bfloat16).reshape(3, 3, channels, channels)
    temporal_grad = (lax.optimization_barrier(jnp.sum(temporal_sums, axis=0)) * grad_scale).astype(jnp.bfloat16).reshape(3, channels, channels)
    return (decoded, input_grad, spatial_grad, temporal_grad)
```

```python
import math

import jax
import jax.numpy as jnp
from jax import lax
from jax.sharding import PartitionSpec as P


def extended(x, sides, width):
    for axis, dim in sides:
        count, length = (lax.axis_size(axis), x.shape[dim])
        up = [(i, (i + 1) % count) for i in range(count - 1)]
        down = [(j, i) for i, j in up]
        last = lax.slice_in_dim(x, length - width, length, axis=dim)
        initial = lax.slice_in_dim(x, 0, width, axis=dim)
        before = lax.ppermute(last, axis, up)
        after = lax.ppermute(initial, axis, down)
        x = jnp.concatenate([before, x, after], axis=dim)
    return x


def from_behind(block, axis, distance):
    devices = range(lax.axis_size(axis))
    route = [(i - distance, i) for i in devices if i - distance in devices]
    return lax.ppermute(block, axis, route)


def silu_slope(values):
    sigmoid_value = jax.nn.sigmoid(values)
    return sigmoid_value * (1.0 + values * (1.0 - sigmoid_value))


def frame_taps(source, frame_count):
    return jnp.concatenate(
        [source[shift_tap : shift_tap + frame_count] for shift_tap in range(3)], axis=-1
    )


def flat_dot(left_side, right_side):
    return jnp.dot(
        left_side.reshape(-1, left_side.shape[-1]), right_side, preferred_element_type=jnp.float32
    )


def local(frames_in, cotangent, w_spatial, w_temporal):
    inputs = frames_in[0]
    upstream = cotangent[0]
    frame_count, row_count, col_count, channels = inputs.shape
    temporal_flat = w_temporal.reshape(3 * channels, channels)
    temporal_back = jnp.concatenate([w_temporal[2].T, w_temporal[1].T, w_temporal[0].T], axis=0)
    first_shard = lax.axis_index("tm") == 0
    activated = jax.nn.silu(inputs.astype(jnp.float32)).astype(jnp.bfloat16)
    activ_rows = extended(activated, (("height", 1),), 1)
    activ_pad = jnp.pad(activ_rows, ((0, 0), (0, 0), (1, 1), (0, 0)))
    spatial_out = lax.conv_general_dilated(
        activ_pad, w_spatial, (1, 1), "VALID", dimension_numbers=("NHWC", "HWIO", "NHWC"),
        preferred_element_type=jnp.float32,
    ).astype(jnp.bfloat16)
    earlier = from_behind(spatial_out[frame_count - 2 :], "tm", 1)
    repeated = jnp.broadcast_to(spatial_out[:1], earlier.shape)
    earlier = jnp.where(first_shard, repeated, earlier)
    padded_frames = jnp.concatenate([earlier, spatial_out], axis=0)
    frame_stack = frame_taps(padded_frames, frame_count).reshape(-1, 3 * channels)
    temporal_out = jnp.dot(frame_stack, temporal_flat, preferred_element_type=jnp.float32).reshape(
        inputs.shape
    )
    decoded = (inputs.astype(jnp.float32) + temporal_out).astype(jnp.bfloat16)
    upstream_ext = jnp.pad(upstream, ((2, 2), (0, 0), (0, 0), (0, 0)))
    frame_part = flat_dot(frame_taps(upstream_ext, frame_count + 2), temporal_back)
    frame_part = frame_part.reshape(frame_count + 2, row_count, col_count, channels)
    rim_part = frame_part[:2]
    returned = from_behind(rim_part, "tm", -1)
    frame_sum = frame_part[2:]
    frame_sum = frame_sum.at[frame_count - 2 :].add(returned)
    frame_sum = frame_sum.at[0].add(jnp.where(first_shard, rim_part[0] + rim_part[1], 0.0))
    frame_grad = frame_sum.astype(jnp.bfloat16)
    grad_pad = jnp.pad(frame_grad, ((0, 0), (2, 2), (1, 1), (0, 0)))
    spatial_flip = jnp.flip(w_spatial, (0, 1)).transpose(0, 1, 3, 2)
    grad_ext = lax.conv_general_dilated(
        grad_pad, spatial_flip, (1, 1), "VALID", dimension_numbers=("NHWC", "HWIO", "NHWC"),
        preferred_element_type=jnp.float32,
    )
    edge_rows = jnp.stack([grad_ext[:, 0], grad_ext[:, row_count + 1]], axis=1)
    arrived = extended(edge_rows.astype(jnp.bfloat16), (("height", 1),), 1).astype(edge_rows.dtype)
    act_grad = grad_ext[:, 1 : row_count + 1]
    act_grad = act_grad.at[:, 0].add(arrived[:, 0])
    act_grad = act_grad.at[:, row_count - 1].add(arrived[:, 3])
    input_grad = (
        upstream.astype(jnp.float32) + silu_slope(inputs.astype(jnp.float32)) * act_grad
    ).astype(jnp.bfloat16)
    cell_count = (
        frame_count
        * lax.axis_size("tm")
        * row_count
        * lax.axis_size("height")
        * col_count
        * lax.axis_size("dp")
    )
    grad_scale = 1.0 / math.sqrt(cell_count)
    contract = (((0,), (0,)), ((), ()))
    spatial_term = lax.conv_general_dilated(
        activ_pad, frame_grad, (1, 1), "VALID", dimension_numbers=("CHWN", "IHWO", "HWNC"),
        preferred_element_type=jnp.float32,
    ).reshape(9 * channels, channels)
    temporal_term = lax.dot_general(
        frame_stack, upstream.reshape(-1, channels), contract, preferred_element_type=jnp.float32
    )
    weight_terms = jnp.concatenate([spatial_term, temporal_term], axis=0) * grad_scale
    summed = lax.psum(weight_terms, ("tm", "height", "dp")).astype(jnp.bfloat16)
    spatial_grad = summed[: 9 * channels].reshape(3, 3, channels, channels)
    temporal_grad = summed[9 * channels :].reshape(3, channels, channels)
    return (decoded[None], input_grad[None], spatial_grad, temporal_grad)


def solution(mesh):
    return jax.shard_map(
        local,
        mesh=mesh,
        in_specs=(
            P("dp", "tm", "height", None, None),
            P("dp", "tm", "height", None, None),
            P(),
            P(),
        ),
        out_specs=(
            P("dp", "tm", "height", None, None),
            P("dp", "tm", "height", None, None),
            P(),
            P(),
        ),
        check_vma=False,
    )
```

```python
import math

import jax
import jax.numpy as jnp
from jax import lax
from jax.sharding import PartitionSpec as P


def extended(x, sides, width):
    for axis, dim in sides:
        count, length = (lax.axis_size(axis), x.shape[dim])
        up = [(i, (i + 1) % count) for i in range(count - 1)]
        down = [(j, i) for i, j in up]
        last = lax.slice_in_dim(x, length - width, length, axis=dim)
        initial = lax.slice_in_dim(x, 0, width, axis=dim)
        before = lax.ppermute(last, axis, up)
        after = lax.ppermute(initial, axis, down)
        x = jnp.concatenate([before, x, after], axis=dim)
    return x


def from_behind(block, axis, distance):
    devices = range(lax.axis_size(axis))
    route = [(i - distance, i) for i in devices if i - distance in devices]
    return lax.ppermute(block, axis, route)


def silu_slope(values):
    sigmoid_value = jax.nn.sigmoid(values)
    return sigmoid_value * (1.0 + values * (1.0 - sigmoid_value))


def forward_taps(padded, row_count, col_count):
    pieces = [
        padded[:, row_tap : row_tap + row_count, col_tap : col_tap + col_count]
        for row_tap in range(3)
        for col_tap in range(3)
    ]
    return jnp.concatenate(pieces, axis=-1)


def backward_taps(padded, row_count, col_count):
    pieces = [
        padded[:, 2 - row_tap : 2 - row_tap + row_count, 2 - col_tap : 2 - col_tap + col_count]
        for row_tap in range(3)
        for col_tap in range(3)
    ]
    return jnp.concatenate(pieces, axis=-1)


def frame_taps(source, frame_count):
    return jnp.concatenate(
        [source[shift_tap : shift_tap + frame_count] for shift_tap in range(3)], axis=-1
    )


def flat_dot(left_side, right_side):
    return jnp.dot(
        left_side.reshape(-1, left_side.shape[-1]), right_side, preferred_element_type=jnp.float32
    )


def local(frames_in, cotangent, w_spatial, w_temporal):
    inputs = frames_in[0]
    upstream = cotangent[0]
    frame_count, row_count, col_count, channels = inputs.shape
    spatial_flat = w_spatial.reshape(9 * channels, channels)
    temporal_flat = w_temporal.reshape(3 * channels, channels)
    spatial_back = jnp.concatenate(
        [w_spatial[row_tap, col_tap].T for row_tap in range(3) for col_tap in range(3)], axis=0
    )
    temporal_back = jnp.concatenate([w_temporal[2].T, w_temporal[1].T, w_temporal[0].T], axis=0)
    first_shard = lax.axis_index("tm") == 0
    activated = jax.nn.silu(inputs.astype(jnp.float32)).astype(jnp.bfloat16)
    activ_rows = extended(activated, (("height", 1),), 1)
    activ_pad = jnp.pad(activ_rows, ((0, 0), (0, 0), (1, 1), (0, 0)))
    activ_taps = forward_taps(activ_pad, row_count, col_count).reshape(-1, 9 * channels)
    spatial_out = jnp.dot(activ_taps, spatial_flat, preferred_element_type=jnp.float32)
    spatial_out = spatial_out.astype(jnp.bfloat16).reshape(inputs.shape)
    earlier = from_behind(spatial_out[frame_count - 2 :], "tm", 1)
    repeated = jnp.broadcast_to(spatial_out[:1], earlier.shape)
    earlier = jnp.where(first_shard, repeated, earlier)
    padded_frames = jnp.concatenate([earlier, spatial_out], axis=0)
    frame_stack = frame_taps(padded_frames, frame_count).reshape(-1, 3 * channels)
    temporal_out = jnp.dot(frame_stack, temporal_flat, preferred_element_type=jnp.float32).reshape(
        inputs.shape
    )
    decoded = (inputs.astype(jnp.float32) + temporal_out).astype(jnp.bfloat16)
    upstream_ext = jnp.pad(upstream, ((2, 2), (0, 0), (0, 0), (0, 0)))
    frame_part = flat_dot(frame_taps(upstream_ext, frame_count + 2), temporal_back)
    frame_part = frame_part.reshape(frame_count + 2, row_count, col_count, channels)
    rim_part = frame_part[:2]
    returned = from_behind(rim_part, "tm", -1)
    frame_sum = frame_part[2:]
    frame_sum = frame_sum.at[frame_count - 2 :].add(returned)
    frame_sum = frame_sum.at[0].add(jnp.where(first_shard, rim_part[0] + rim_part[1], 0.0))
    frame_grad = frame_sum.astype(jnp.bfloat16)
    grad_pad = jnp.pad(frame_grad, ((0, 0), (2, 2), (1, 1), (0, 0)))
    grad_ext = flat_dot(backward_taps(grad_pad, row_count + 2, col_count), spatial_back)
    grad_ext = grad_ext.reshape(frame_count, row_count + 2, col_count, channels)
    edge_rows = jnp.stack([grad_ext[:, 0], grad_ext[:, row_count + 1]], axis=1).astype(jnp.bfloat16)
    cell_count = (
        frame_count
        * lax.axis_size("tm")
        * row_count
        * lax.axis_size("height")
        * col_count
        * lax.axis_size("dp")
    )
    grad_scale = 1.0 / math.sqrt(cell_count)
    contract = (((0,), (0,)), ((), ()))
    spatial_term = lax.dot_general(
        activ_taps, frame_grad.reshape(-1, channels), contract, preferred_element_type=jnp.float32
    )
    temporal_term = lax.dot_general(
        frame_stack, upstream.reshape(-1, channels), contract, preferred_element_type=jnp.float32
    )
    weight_terms = jnp.concatenate([spatial_term, temporal_term], axis=0) * grad_scale
    weight_terms, edge_rows = lax.optimization_barrier((weight_terms, edge_rows))
    summed = lax.psum(weight_terms, ("tm", "height", "dp")).astype(jnp.bfloat16)
    arrived = extended(edge_rows, (("height", 1),), 1).astype(jnp.float32)
    act_grad = grad_ext[:, 1 : row_count + 1]
    act_grad = act_grad.at[:, 0].add(arrived[:, 0])
    act_grad = act_grad.at[:, row_count - 1].add(arrived[:, 3])
    input_grad = (
        upstream.astype(jnp.float32) + silu_slope(inputs.astype(jnp.float32)) * act_grad
    ).astype(jnp.bfloat16)
    spatial_grad = summed[: 9 * channels].reshape(3, 3, channels, channels)
    temporal_grad = summed[9 * channels :].reshape(3, channels, channels)
    return (decoded[None], input_grad[None], spatial_grad, temporal_grad)


def solution(mesh):
    return jax.shard_map(
        local,
        mesh=mesh,
        in_specs=(
            P("dp", "tm", "height", None, None),
            P("dp", "tm", "height", None, None),
            P(),
            P(),
        ),
        out_specs=(
            P("dp", "tm", "height", None, None),
            P("dp", "tm", "height", None, None),
            P(),
            P(),
        ),
        check_vma=False,
    )
```

```python
import math

import jax
import jax.numpy as jnp
from jax import lax
from jax.sharding import PartitionSpec as P


def extended(x, sides, width):
    for axis, dim in sides:
        count, length = (lax.axis_size(axis), x.shape[dim])
        up = [(i, (i + 1) % count) for i in range(count - 1)]
        down = [(j, i) for i, j in up]
        last = lax.slice_in_dim(x, length - width, length, axis=dim)
        initial = lax.slice_in_dim(x, 0, width, axis=dim)
        before = lax.ppermute(last, axis, up)
        after = lax.ppermute(initial, axis, down)
        x = jnp.concatenate([before, x, after], axis=dim)
    return x


def from_behind(block, axis, distance):
    devices = range(lax.axis_size(axis))
    route = [(i - distance, i) for i in devices if i - distance in devices]
    return lax.ppermute(block, axis, route)


def silu_slope(values):
    sigmoid_value = jax.nn.sigmoid(values)
    return sigmoid_value * (1.0 + values * (1.0 - sigmoid_value))


def forward_taps(padded, row_count, col_count):
    pieces = [
        padded[:, row_tap : row_tap + row_count, col_tap : col_tap + col_count]
        for row_tap in range(3)
        for col_tap in range(3)
    ]
    return jnp.concatenate(pieces, axis=-1)


def backward_taps(padded, row_count, col_count):
    pieces = [
        padded[:, 2 - row_tap : 2 - row_tap + row_count, 2 - col_tap : 2 - col_tap + col_count]
        for row_tap in range(3)
        for col_tap in range(3)
    ]
    return jnp.concatenate(pieces, axis=-1)


def frame_taps(source, frame_count):
    return jnp.concatenate(
        [source[shift_tap : shift_tap + frame_count] for shift_tap in range(3)], axis=-1
    )


def flat_dot(left_side, right_side):
    return jnp.dot(
        left_side.reshape(-1, left_side.shape[-1]), right_side, preferred_element_type=jnp.float32
    )


def local(frames_in, cotangent, w_spatial, w_temporal):
    inputs = frames_in[0]
    upstream = cotangent[0]
    frame_count, row_count, col_count, channels = inputs.shape
    spatial_flat = w_spatial.reshape(9 * channels, channels)
    temporal_flat = w_temporal.reshape(3 * channels, channels)
    spatial_back = jnp.concatenate(
        [w_spatial[row_tap, col_tap].T for row_tap in range(3) for col_tap in range(3)], axis=0
    )
    temporal_back = jnp.concatenate([w_temporal[2].T, w_temporal[1].T, w_temporal[0].T], axis=0)
    first_shard = lax.axis_index("tm") == 0
    inputs_prev = from_behind(inputs[frame_count - 2 :], "tm", 1)
    upstream_next = from_behind(upstream[:2], "tm", -1)
    both = jnp.concatenate(
        [
            jnp.concatenate([inputs_prev, inputs], axis=0),
            jnp.concatenate([upstream, upstream_next], axis=0),
        ],
        axis=-1,
    )
    both = extended(both, (("height", 1),), 1)
    inputs_full = both[..., :channels]
    upstream_full = both[..., channels:]
    activated = jax.nn.silu(inputs_full.astype(jnp.float32)).astype(jnp.bfloat16)
    activ_pad = jnp.pad(activated, ((0, 0), (0, 0), (1, 1), (0, 0)))
    activ_taps = forward_taps(activ_pad, row_count, col_count)
    spatial_all = flat_dot(activ_taps, spatial_flat).astype(jnp.bfloat16)
    spatial_all = spatial_all.reshape(frame_count + 2, row_count, col_count, channels)
    spatial_out = spatial_all[2:]
    repeated = jnp.broadcast_to(spatial_out[:1], (2,) + spatial_out.shape[1:])
    earlier = jnp.where(first_shard, repeated, spatial_all[:2])
    padded_frames = jnp.concatenate([earlier, spatial_out], axis=0)
    frame_stack = frame_taps(padded_frames, frame_count).reshape(-1, 3 * channels)
    temporal_out = jnp.dot(frame_stack, temporal_flat, preferred_element_type=jnp.float32).reshape(
        inputs.shape
    )
    decoded = (inputs.astype(jnp.float32) + temporal_out).astype(jnp.bfloat16)
    frame_sum = flat_dot(frame_taps(upstream_full, frame_count), temporal_back)
    first_up = upstream_full[0].reshape(-1, channels)
    second_up = upstream_full[1].reshape(-1, channels)
    fold_term = jnp.dot(first_up, w_temporal[0].T, preferred_element_type=jnp.float32)
    fold_term = fold_term + jnp.dot(first_up, w_temporal[1].T, preferred_element_type=jnp.float32)
    fold_term = fold_term + jnp.dot(second_up, w_temporal[0].T, preferred_element_type=jnp.float32)
    fold_rows = frame_sum.shape[0] // frame_count
    frame_sum = frame_sum.reshape(frame_count, fold_rows, channels)
    frame_sum = frame_sum.at[0].add(jnp.where(first_shard, fold_term, 0.0))
    frame_grad_full = frame_sum.astype(jnp.bfloat16).reshape(
        frame_count, row_count + 2, col_count, channels
    )
    grad_pad = jnp.pad(frame_grad_full, ((0, 0), (0, 0), (1, 1), (0, 0)))
    act_grad = flat_dot(backward_taps(grad_pad, row_count, col_count), spatial_back)
    act_grad = act_grad.reshape(inputs.shape)
    input_grad = (
        upstream.astype(jnp.float32) + silu_slope(inputs.astype(jnp.float32)) * act_grad
    ).astype(jnp.bfloat16)
    frame_grad = frame_grad_full[:, 1 : row_count + 1]
    cell_count = (
        frame_count
        * lax.axis_size("tm")
        * row_count
        * lax.axis_size("height")
        * col_count
        * lax.axis_size("dp")
    )
    grad_scale = 1.0 / math.sqrt(cell_count)
    contract = (((0,), (0,)), ((), ()))
    local_taps = activ_taps[2:].reshape(-1, 9 * channels)
    spatial_term = lax.dot_general(
        local_taps, frame_grad.reshape(-1, channels), contract, preferred_element_type=jnp.float32
    )
    temporal_term = lax.dot_general(
        frame_stack, upstream.reshape(-1, channels), contract, preferred_element_type=jnp.float32
    )
    weight_terms = jnp.concatenate([spatial_term, temporal_term], axis=0) * grad_scale
    summed = lax.psum(weight_terms, ("tm", "height", "dp")).astype(jnp.bfloat16)
    spatial_grad = summed[: 9 * channels].reshape(3, 3, channels, channels)
    temporal_grad = summed[9 * channels :].reshape(3, channels, channels)
    return (decoded[None], input_grad[None], spatial_grad, temporal_grad)


def solution(mesh):
    return jax.shard_map(
        local,
        mesh=mesh,
        in_specs=(
            P("dp", "tm", "height", None, None),
            P("dp", "tm", "height", None, None),
            P(),
            P(),
        ),
        out_specs=(
            P("dp", "tm", "height", None, None),
            P("dp", "tm", "height", None, None),
            P(),
            P(),
        ),
        check_vma=False,
    )
```

```python
import math

import jax
import jax.numpy as jnp
from jax import lax
from jax.sharding import PartitionSpec as P


def extended(x, sides, width):
    for axis, dim in sides:
        count, length = (lax.axis_size(axis), x.shape[dim])
        up = [(i, (i + 1) % count) for i in range(count - 1)]
        down = [(j, i) for i, j in up]
        last = lax.slice_in_dim(x, length - width, length, axis=dim)
        initial = lax.slice_in_dim(x, 0, width, axis=dim)
        before = lax.ppermute(last, axis, up)
        after = lax.ppermute(initial, axis, down)
        x = jnp.concatenate([before, x, after], axis=dim)
    return x


def from_behind(block, axis, distance):
    devices = range(lax.axis_size(axis))
    route = [(i - distance, i) for i in devices if i - distance in devices]
    return lax.ppermute(block, axis, route)


def silu_slope(values):
    sigmoid_value = jax.nn.sigmoid(values)
    return sigmoid_value * (1.0 + values * (1.0 - sigmoid_value))


def forward_taps(padded, row_count, col_count):
    pieces = [
        padded[:, row_tap : row_tap + row_count, col_tap : col_tap + col_count]
        for row_tap in range(3)
        for col_tap in range(3)
    ]
    return jnp.concatenate(pieces, axis=-1)


def backward_taps(padded, row_count, col_count):
    pieces = [
        padded[:, 2 - row_tap : 2 - row_tap + row_count, 2 - col_tap : 2 - col_tap + col_count]
        for row_tap in range(3)
        for col_tap in range(3)
    ]
    return jnp.concatenate(pieces, axis=-1)


def frame_taps(source, frame_count):
    return jnp.concatenate(
        [source[shift_tap : shift_tap + frame_count] for shift_tap in range(3)], axis=-1
    )


def flat_dot(left_side, right_side):
    return jnp.dot(
        left_side.reshape(-1, left_side.shape[-1]), right_side, preferred_element_type=jnp.float32
    )


def local(frames_in, cotangent, w_spatial, w_temporal):
    inputs = frames_in[0]
    upstream = cotangent[0]
    frame_count, row_count, col_count, channels = inputs.shape
    spatial_flat = w_spatial.reshape(9 * channels, channels)
    temporal_flat = w_temporal.reshape(3 * channels, channels)
    spatial_back = jnp.concatenate(
        [w_spatial[row_tap, col_tap].T for row_tap in range(3) for col_tap in range(3)], axis=0
    )
    temporal_back = jnp.concatenate([w_temporal[2].T, w_temporal[1].T, w_temporal[0].T], axis=0)
    first_shard = lax.axis_index("tm") == 0
    inputs_prev = from_behind(inputs[frame_count - 2 :], "tm", 1)
    upstream_next = from_behind(upstream[:2], "tm", -1)
    local_both = extended(jnp.concatenate([inputs, upstream], axis=-1), (("height", 1),), 1)
    rim_both = extended(
        jnp.concatenate([inputs_prev, upstream_next], axis=-1), (("height", 1),), 1
    )

    def spatial_forward(block):
        activ = jax.nn.silu(block.astype(jnp.float32)).astype(jnp.bfloat16)
        taps = forward_taps(jnp.pad(activ, ((0, 0), (0, 0), (1, 1), (0, 0))), row_count, col_count)
        out = flat_dot(taps, spatial_flat).astype(jnp.bfloat16)
        return taps, out.reshape(block.shape[0], row_count, col_count, channels)

    activ_taps, spatial_out = spatial_forward(local_both[..., :channels])
    unused, spatial_rim = spatial_forward(rim_both[..., :channels])
    repeated = jnp.broadcast_to(spatial_out[:1], (2,) + spatial_out.shape[1:])
    earlier = jnp.where(first_shard, repeated, spatial_rim)
    padded_frames = jnp.concatenate([earlier, spatial_out], axis=0)
    frame_stack = frame_taps(padded_frames, frame_count).reshape(-1, 3 * channels)
    temporal_out = jnp.dot(frame_stack, temporal_flat, preferred_element_type=jnp.float32).reshape(
        inputs.shape
    )
    decoded = (inputs.astype(jnp.float32) + temporal_out).astype(jnp.bfloat16)

    def frame_gradient(source):
        rows = source.shape[1]
        part = flat_dot(frame_taps(source, frame_count), temporal_back)
        first_up = source[0].reshape(-1, channels)
        second_up = source[1].reshape(-1, channels)
        fold = jnp.dot(first_up, w_temporal[0].T, preferred_element_type=jnp.float32)
        fold = fold + jnp.dot(first_up, w_temporal[1].T, preferred_element_type=jnp.float32)
        fold = fold + jnp.dot(second_up, w_temporal[0].T, preferred_element_type=jnp.float32)
        part = part.reshape(frame_count, rows * col_count, channels)
        part = part.at[0].add(jnp.where(first_shard, fold, 0.0))
        return part.astype(jnp.bfloat16).reshape(frame_count, rows, col_count, channels)

    frame_grad = frame_gradient(jnp.concatenate([upstream, upstream_next], axis=0))
    up_rows = jnp.concatenate([local_both[..., channels:], rim_both[..., channels:]], axis=0)
    edge_grad = frame_gradient(jnp.stack([up_rows[:, 0], up_rows[:, row_count + 1]], axis=1))
    frame_grad_full = jnp.concatenate([edge_grad[:, :1], frame_grad, edge_grad[:, 1:]], axis=1)
    grad_pad = jnp.pad(frame_grad_full, ((0, 0), (0, 0), (1, 1), (0, 0)))
    act_grad = flat_dot(backward_taps(grad_pad, row_count, col_count), spatial_back)
    act_grad = act_grad.reshape(inputs.shape)
    input_grad = (
        upstream.astype(jnp.float32) + silu_slope(inputs.astype(jnp.float32)) * act_grad
    ).astype(jnp.bfloat16)
    cell_count = (
        frame_count
        * lax.axis_size("tm")
        * row_count
        * lax.axis_size("height")
        * col_count
        * lax.axis_size("dp")
    )
    grad_scale = 1.0 / math.sqrt(cell_count)
    contract = (((0,), (0,)), ((), ()))
    local_taps = activ_taps.reshape(-1, 9 * channels)
    spatial_term = lax.dot_general(
        local_taps, frame_grad.reshape(-1, channels), contract, preferred_element_type=jnp.float32
    )
    temporal_term = lax.dot_general(
        frame_stack, upstream.reshape(-1, channels), contract, preferred_element_type=jnp.float32
    )
    weight_terms = jnp.concatenate([spatial_term, temporal_term], axis=0) * grad_scale
    summed = lax.psum(weight_terms, ("tm", "height", "dp")).astype(jnp.bfloat16)
    spatial_grad = summed[: 9 * channels].reshape(3, 3, channels, channels)
    temporal_grad = summed[9 * channels :].reshape(3, channels, channels)
    return (decoded[None], input_grad[None], spatial_grad, temporal_grad)


def solution(mesh):
    return jax.shard_map(
        local,
        mesh=mesh,
        in_specs=(
            P("dp", "tm", "height", None, None),
            P("dp", "tm", "height", None, None),
            P(),
            P(),
        ),
        out_specs=(
            P("dp", "tm", "height", None, None),
            P("dp", "tm", "height", None, None),
            P(),
            P(),
        ),
        check_vma=False,
    )
```

```python
import math

import jax
import jax.numpy as jnp
from jax import lax
from jax.sharding import PartitionSpec as P


def extended(x, sides, width):
    for axis, dim in sides:
        count, length = (lax.axis_size(axis), x.shape[dim])
        up = [(i, (i + 1) % count) for i in range(count - 1)]
        down = [(j, i) for i, j in up]
        last = lax.slice_in_dim(x, length - width, length, axis=dim)
        initial = lax.slice_in_dim(x, 0, width, axis=dim)
        before = lax.ppermute(last, axis, up)
        after = lax.ppermute(initial, axis, down)
        x = jnp.concatenate([before, x, after], axis=dim)
    return x


def from_behind(block, axis, distance):
    devices = range(lax.axis_size(axis))
    route = [(i - distance, i) for i in devices if i - distance in devices]
    return lax.ppermute(block, axis, route)


def silu_slope(values):
    sigmoid_value = jax.nn.sigmoid(values)
    return sigmoid_value * (1.0 + values * (1.0 - sigmoid_value))


def forward_taps(padded, row_count, col_count):
    pieces = [
        padded[:, row_tap : row_tap + row_count, col_tap : col_tap + col_count]
        for row_tap in range(3)
        for col_tap in range(3)
    ]
    return jnp.concatenate(pieces, axis=-1)


def backward_taps(padded, row_count, col_count):
    pieces = [
        padded[:, 2 - row_tap : 2 - row_tap + row_count, 2 - col_tap : 2 - col_tap + col_count]
        for row_tap in range(3)
        for col_tap in range(3)
    ]
    return jnp.concatenate(pieces, axis=-1)


def frame_taps(source, frame_count):
    return jnp.concatenate(
        [source[shift_tap : shift_tap + frame_count] for shift_tap in range(3)], axis=-1
    )


def flat_dot(left_side, right_side):
    return jnp.dot(
        left_side.reshape(-1, left_side.shape[-1]), right_side, preferred_element_type=jnp.float32
    )


def local(frames_in, cotangent, w_spatial, w_temporal):
    inputs = frames_in[0]
    upstream = cotangent[0]
    frame_count, row_count, col_count, channels = inputs.shape
    spatial_flat = w_spatial.reshape(9 * channels, channels)
    temporal_flat = w_temporal.reshape(3 * channels, channels)
    spatial_back = jnp.concatenate(
        [w_spatial[row_tap, col_tap].T for row_tap in range(3) for col_tap in range(3)], axis=0
    )
    temporal_back = jnp.concatenate([w_temporal[2].T, w_temporal[1].T, w_temporal[0].T], axis=0)
    first_shard = lax.axis_index("tm") == 0
    inputs_prev = from_behind(inputs[frame_count - 2 :], "tm", 1)
    upstream_next = from_behind(upstream[:2], "tm", -1)
    local_both = extended(jnp.concatenate([inputs, upstream], axis=-1), (("height", 1),), 1)

    def spatial_forward(block):
        activ = jax.nn.silu(block.astype(jnp.float32)).astype(jnp.bfloat16)
        taps = forward_taps(jnp.pad(activ, ((0, 0), (0, 0), (1, 1), (0, 0))), row_count, col_count)
        out = flat_dot(taps, spatial_flat).astype(jnp.bfloat16)
        return taps, out.reshape(block.shape[0], row_count, col_count, channels)

    def frame_gradient(source):
        rows = source.shape[1]
        part = flat_dot(frame_taps(source, frame_count), temporal_back)
        first_up = source[0].reshape(-1, channels)
        second_up = source[1].reshape(-1, channels)
        fold = jnp.dot(first_up, w_temporal[0].T, preferred_element_type=jnp.float32)
        fold = fold + jnp.dot(first_up, w_temporal[1].T, preferred_element_type=jnp.float32)
        fold = fold + jnp.dot(second_up, w_temporal[0].T, preferred_element_type=jnp.float32)
        part = part.reshape(frame_count, rows * col_count, channels)
        part = part.at[0].add(jnp.where(first_shard, fold, 0.0))
        return part.astype(jnp.bfloat16).reshape(frame_count, rows, col_count, channels)

    activ_taps, spatial_out = spatial_forward(local_both[..., :channels])
    frame_grad = frame_gradient(jnp.concatenate([upstream, upstream_next], axis=0))
    contract = (((0,), (0,)), ((), ()))
    spatial_term = lax.dot_general(
        activ_taps.reshape(-1, 9 * channels),
        frame_grad.reshape(-1, channels),
        contract,
        preferred_element_type=jnp.float32,
    )
    rim_source = jnp.concatenate([inputs_prev, upstream_next], axis=-1)
    spatial_out, spatial_term, rim_source = lax.optimization_barrier(
        (spatial_out, spatial_term, rim_source)
    )
    rim_both = extended(rim_source, (("height", 1),), 1)
    unused, spatial_rim = spatial_forward(rim_both[..., :channels])
    repeated = jnp.broadcast_to(spatial_out[:1], (2,) + spatial_out.shape[1:])
    earlier = jnp.where(first_shard, repeated, spatial_rim)
    padded_frames = jnp.concatenate([earlier, spatial_out], axis=0)
    frame_stack = frame_taps(padded_frames, frame_count).reshape(-1, 3 * channels)
    temporal_out = jnp.dot(frame_stack, temporal_flat, preferred_element_type=jnp.float32).reshape(
        inputs.shape
    )
    decoded = (inputs.astype(jnp.float32) + temporal_out).astype(jnp.bfloat16)

    up_rows = jnp.concatenate([local_both[..., channels:], rim_both[..., channels:]], axis=0)
    edge_grad = frame_gradient(jnp.stack([up_rows[:, 0], up_rows[:, row_count + 1]], axis=1))
    frame_grad_full = jnp.concatenate([edge_grad[:, :1], frame_grad, edge_grad[:, 1:]], axis=1)
    grad_pad = jnp.pad(frame_grad_full, ((0, 0), (0, 0), (1, 1), (0, 0)))
    act_grad = flat_dot(backward_taps(grad_pad, row_count, col_count), spatial_back)
    act_grad = act_grad.reshape(inputs.shape)
    input_grad = (
        upstream.astype(jnp.float32) + silu_slope(inputs.astype(jnp.float32)) * act_grad
    ).astype(jnp.bfloat16)
    cell_count = (
        frame_count
        * lax.axis_size("tm")
        * row_count
        * lax.axis_size("height")
        * col_count
        * lax.axis_size("dp")
    )
    grad_scale = 1.0 / math.sqrt(cell_count)
    temporal_term = lax.dot_general(
        frame_stack, upstream.reshape(-1, channels), contract, preferred_element_type=jnp.float32
    )
    weight_terms = jnp.concatenate([spatial_term, temporal_term], axis=0) * grad_scale
    summed = lax.psum(weight_terms, ("tm", "height", "dp")).astype(jnp.bfloat16)
    spatial_grad = summed[: 9 * channels].reshape(3, 3, channels, channels)
    temporal_grad = summed[9 * channels :].reshape(3, channels, channels)
    return (decoded[None], input_grad[None], spatial_grad, temporal_grad)


def solution(mesh):
    return jax.shard_map(
        local,
        mesh=mesh,
        in_specs=(
            P("dp", "tm", "height", None, None),
            P("dp", "tm", "height", None, None),
            P(),
            P(),
        ),
        out_specs=(
            P("dp", "tm", "height", None, None),
            P("dp", "tm", "height", None, None),
            P(),
            P(),
        ),
        check_vma=False,
    )
```

```python
import math

import jax
import jax.numpy as jnp
from jax import lax
from jax.sharding import PartitionSpec as P


def extended(x, sides, width):
    for axis, dim in sides:
        count, length = (lax.axis_size(axis), x.shape[dim])
        up = [(i, (i + 1) % count) for i in range(count - 1)]
        down = [(j, i) for i, j in up]
        last = lax.slice_in_dim(x, length - width, length, axis=dim)
        initial = lax.slice_in_dim(x, 0, width, axis=dim)
        before = lax.ppermute(last, axis, up)
        after = lax.ppermute(initial, axis, down)
        x = jnp.concatenate([before, x, after], axis=dim)
    return x


def from_behind(block, axis, distance):
    devices = range(lax.axis_size(axis))
    route = [(i - distance, i) for i in devices if i - distance in devices]
    return lax.ppermute(block, axis, route)


def silu_slope(values):
    sigmoid_value = jax.nn.sigmoid(values)
    return sigmoid_value * (1.0 + values * (1.0 - sigmoid_value))


def forward_taps(padded, row_count, col_count):
    pieces = [
        padded[:, row_tap : row_tap + row_count, col_tap : col_tap + col_count]
        for row_tap in range(3)
        for col_tap in range(3)
    ]
    return jnp.concatenate(pieces, axis=-1)


def backward_taps(padded, row_count, col_count):
    pieces = [
        padded[:, 2 - row_tap : 2 - row_tap + row_count, 2 - col_tap : 2 - col_tap + col_count]
        for row_tap in range(3)
        for col_tap in range(3)
    ]
    return jnp.concatenate(pieces, axis=-1)


def frame_taps(source, frame_count):
    return jnp.concatenate(
        [source[shift_tap : shift_tap + frame_count] for shift_tap in range(3)], axis=-1
    )


def flat_dot(left_side, right_side):
    return jnp.dot(
        left_side.reshape(-1, left_side.shape[-1]), right_side, preferred_element_type=jnp.float32
    )


def local(frames_in, cotangent, w_spatial, w_temporal):
    inputs = frames_in[0]
    upstream = cotangent[0]
    frame_count, row_count, col_count, channels = inputs.shape
    spatial_flat = w_spatial.reshape(9 * channels, channels)
    temporal_flat = w_temporal.reshape(3 * channels, channels)
    spatial_back = jnp.concatenate(
        [w_spatial[row_tap, col_tap].T for row_tap in range(3) for col_tap in range(3)], axis=0
    )
    temporal_back = jnp.concatenate([w_temporal[2].T, w_temporal[1].T, w_temporal[0].T], axis=0)
    first_shard = lax.axis_index("tm") == 0
    inputs_prev = from_behind(inputs[frame_count - 2 :], "tm", 1)
    upstream_next = from_behind(upstream[:2], "tm", -1)
    local_both = extended(jnp.concatenate([inputs, upstream], axis=-1), (("height", 1),), 1)
    rim_both = extended(
        jnp.concatenate([inputs_prev, upstream_next], axis=-1), (("height", 1),), 1
    )

    def spatial_forward(block):
        activ = jax.nn.silu(block.astype(jnp.float32)).astype(jnp.bfloat16)
        taps = forward_taps(jnp.pad(activ, ((0, 0), (0, 0), (1, 1), (0, 0))), row_count, col_count)
        out = flat_dot(taps, spatial_flat).astype(jnp.bfloat16)
        return taps, out.reshape(block.shape[0], row_count, col_count, channels)

    activ_taps, spatial_out = spatial_forward(local_both[..., :channels])
    unused, spatial_rim = spatial_forward(rim_both[..., :channels])
    repeated = jnp.broadcast_to(spatial_out[:1], (2,) + spatial_out.shape[1:])
    earlier = jnp.where(first_shard, repeated, spatial_rim)
    padded_frames = jnp.concatenate([earlier, spatial_out], axis=0)
    frame_stack = frame_taps(padded_frames, frame_count).reshape(-1, 3 * channels)
    temporal_out = jnp.dot(frame_stack, temporal_flat, preferred_element_type=jnp.float32).reshape(
        inputs.shape
    )
    decoded = (inputs.astype(jnp.float32) + temporal_out).astype(jnp.bfloat16)

    def frame_gradient(source):
        rows = source.shape[1]
        part = flat_dot(frame_taps(source, frame_count), temporal_back)
        first_up = source[0].reshape(-1, channels)
        second_up = source[1].reshape(-1, channels)
        fold = jnp.dot(first_up, w_temporal[0].T, preferred_element_type=jnp.float32)
        fold = fold + jnp.dot(first_up, w_temporal[1].T, preferred_element_type=jnp.float32)
        fold = fold + jnp.dot(second_up, w_temporal[0].T, preferred_element_type=jnp.float32)
        part = part.reshape(frame_count, rows * col_count, channels)
        part = part.at[0].add(jnp.where(first_shard, fold, 0.0))
        return part.astype(jnp.bfloat16).reshape(frame_count, rows, col_count, channels)

    frame_grad = frame_gradient(jnp.concatenate([upstream, upstream_next], axis=0))
    up_rows = jnp.concatenate([local_both[..., channels:], rim_both[..., channels:]], axis=0)
    edge_grad = frame_gradient(jnp.stack([up_rows[:, 0], up_rows[:, row_count + 1]], axis=1))
    grad_pad = jnp.pad(frame_grad, ((0, 0), (1, 1), (1, 1), (0, 0)))
    act_grad = flat_dot(backward_taps(grad_pad, row_count, col_count), spatial_back)
    act_grad = act_grad.reshape(inputs.shape)
    edge_pad = jnp.pad(edge_grad, ((0, 0), (0, 0), (1, 1), (0, 0)))
    edge_pad = jnp.concatenate(
        [edge_pad[:, :1], jnp.zeros_like(edge_pad), edge_pad[:, 1:]], axis=1
    )
    edge_part = flat_dot(backward_taps(edge_pad, 2, col_count), spatial_back)
    edge_part = edge_part.reshape(frame_count, 2, col_count, channels)
    act_grad = act_grad.at[:, 0].add(edge_part[:, 0])
    act_grad = act_grad.at[:, row_count - 1].add(edge_part[:, 1])
    input_grad = (
        upstream.astype(jnp.float32) + silu_slope(inputs.astype(jnp.float32)) * act_grad
    ).astype(jnp.bfloat16)
    cell_count = (
        frame_count
        * lax.axis_size("tm")
        * row_count
        * lax.axis_size("height")
        * col_count
        * lax.axis_size("dp")
    )
    grad_scale = 1.0 / math.sqrt(cell_count)
    contract = (((0,), (0,)), ((), ()))
    local_taps = activ_taps.reshape(-1, 9 * channels)
    spatial_term = lax.dot_general(
        local_taps, frame_grad.reshape(-1, channels), contract, preferred_element_type=jnp.float32
    )
    temporal_term = lax.dot_general(
        frame_stack, upstream.reshape(-1, channels), contract, preferred_element_type=jnp.float32
    )
    weight_terms = jnp.concatenate([spatial_term, temporal_term], axis=0) * grad_scale
    summed = lax.psum(weight_terms, ("tm", "height", "dp")).astype(jnp.bfloat16)
    spatial_grad = summed[: 9 * channels].reshape(3, 3, channels, channels)
    temporal_grad = summed[9 * channels :].reshape(3, channels, channels)
    return (decoded[None], input_grad[None], spatial_grad, temporal_grad)


def solution(mesh):
    return jax.shard_map(
        local,
        mesh=mesh,
        in_specs=(
            P("dp", "tm", "height", None, None),
            P("dp", "tm", "height", None, None),
            P(),
            P(),
        ),
        out_specs=(
            P("dp", "tm", "height", None, None),
            P("dp", "tm", "height", None, None),
            P(),
            P(),
        ),
        check_vma=False,
    )
```

```python
import math

import jax
import jax.numpy as jnp
from jax import lax
from jax.sharding import PartitionSpec as P


def extended(x, sides, width):
    for axis, dim in sides:
        count, length = (lax.axis_size(axis), x.shape[dim])
        up = [(i, (i + 1) % count) for i in range(count - 1)]
        down = [(j, i) for i, j in up]
        last = lax.slice_in_dim(x, length - width, length, axis=dim)
        initial = lax.slice_in_dim(x, 0, width, axis=dim)
        before = lax.ppermute(last, axis, up)
        after = lax.ppermute(initial, axis, down)
        x = jnp.concatenate([before, x, after], axis=dim)
    return x


def from_behind(block, axis, distance):
    devices = range(lax.axis_size(axis))
    route = [(i - distance, i) for i in devices if i - distance in devices]
    return lax.ppermute(block, axis, route)


def diagonal(block, frame_step, row_step):
    frames, rows = (lax.axis_size("tm"), lax.axis_size("height"))
    route = [
        (t * rows + h, (t + frame_step) * rows + h + row_step)
        for t in range(frames)
        for h in range(rows)
        if 0 <= t + frame_step < frames and 0 <= h + row_step < rows
    ]
    return lax.ppermute(block, ("tm", "height"), route)


def silu_slope(values):
    sigmoid_value = jax.nn.sigmoid(values)
    return sigmoid_value * (1.0 + values * (1.0 - sigmoid_value))


def forward_taps(padded, row_count, col_count):
    pieces = [
        padded[:, row_tap : row_tap + row_count, col_tap : col_tap + col_count]
        for row_tap in range(3)
        for col_tap in range(3)
    ]
    return jnp.concatenate(pieces, axis=-1)


def backward_taps(padded, row_count, col_count):
    pieces = [
        padded[:, 2 - row_tap : 2 - row_tap + row_count, 2 - col_tap : 2 - col_tap + col_count]
        for row_tap in range(3)
        for col_tap in range(3)
    ]
    return jnp.concatenate(pieces, axis=-1)


def frame_taps(source, frame_count):
    return jnp.concatenate(
        [source[shift_tap : shift_tap + frame_count] for shift_tap in range(3)], axis=-1
    )


def flat_dot(left_side, right_side):
    return jnp.dot(
        left_side.reshape(-1, left_side.shape[-1]), right_side, preferred_element_type=jnp.float32
    )


def local(frames_in, cotangent, w_spatial, w_temporal):
    inputs = frames_in[0]
    upstream = cotangent[0]
    frame_count, row_count, col_count, channels = inputs.shape
    spatial_flat = w_spatial.reshape(9 * channels, channels)
    temporal_flat = w_temporal.reshape(3 * channels, channels)
    spatial_back = jnp.concatenate(
        [w_spatial[row_tap, col_tap].T for row_tap in range(3) for col_tap in range(3)], axis=0
    )
    temporal_back = jnp.concatenate([w_temporal[2].T, w_temporal[1].T, w_temporal[0].T], axis=0)
    first_shard = lax.axis_index("tm") == 0
    inputs_prev = from_behind(inputs[frame_count - 2 :], "tm", 1)
    upstream_next = from_behind(upstream[:2], "tm", -1)
    local_both = extended(jnp.concatenate([inputs, upstream], axis=-1), (("height", 1),), 1)
    rim_in = jnp.concatenate(
        [
            diagonal(inputs[frame_count - 2 :, row_count - 1 :], 1, 1),
            inputs_prev,
            diagonal(inputs[frame_count - 2 :, :1], 1, -1),
        ],
        axis=1,
    )
    rim_up = jnp.concatenate(
        [
            diagonal(upstream[:2, row_count - 1 :], -1, 1),
            upstream_next,
            diagonal(upstream[:2, :1], -1, -1),
        ],
        axis=1,
    )

    def spatial_forward(block):
        activ = jax.nn.silu(block.astype(jnp.float32)).astype(jnp.bfloat16)
        taps = forward_taps(jnp.pad(activ, ((0, 0), (0, 0), (1, 1), (0, 0))), row_count, col_count)
        out = flat_dot(taps, spatial_flat).astype(jnp.bfloat16)
        return taps, out.reshape(block.shape[0], row_count, col_count, channels)

    activ_taps, spatial_out = spatial_forward(local_both[..., :channels])
    unused, spatial_rim = spatial_forward(rim_in)
    repeated = jnp.broadcast_to(spatial_out[:1], (2,) + spatial_out.shape[1:])
    earlier = jnp.where(first_shard, repeated, spatial_rim)
    padded_frames = jnp.concatenate([earlier, spatial_out], axis=0)
    frame_stack = frame_taps(padded_frames, frame_count).reshape(-1, 3 * channels)
    temporal_out = jnp.dot(frame_stack, temporal_flat, preferred_element_type=jnp.float32).reshape(
        inputs.shape
    )
    decoded = (inputs.astype(jnp.float32) + temporal_out).astype(jnp.bfloat16)

    def frame_gradient(source):
        rows = source.shape[1]
        part = flat_dot(frame_taps(source, frame_count), temporal_back)
        first_up = source[0].reshape(-1, channels)
        second_up = source[1].reshape(-1, channels)
        fold = jnp.dot(first_up, w_temporal[0].T, preferred_element_type=jnp.float32)
        fold = fold + jnp.dot(first_up, w_temporal[1].T, preferred_element_type=jnp.float32)
        fold = fold + jnp.dot(second_up, w_temporal[0].T, preferred_element_type=jnp.float32)
        part = part.reshape(frame_count, rows * col_count, channels)
        part = part.at[0].add(jnp.where(first_shard, fold, 0.0))
        return part.astype(jnp.bfloat16).reshape(frame_count, rows, col_count, channels)

    frame_grad = frame_gradient(jnp.concatenate([upstream, upstream_next], axis=0))
    up_rows = jnp.concatenate([local_both[..., channels:], rim_up], axis=0)
    edge_grad = frame_gradient(jnp.stack([up_rows[:, 0], up_rows[:, row_count + 1]], axis=1))
    frame_grad_full = jnp.concatenate([edge_grad[:, :1], frame_grad, edge_grad[:, 1:]], axis=1)
    grad_pad = jnp.pad(frame_grad_full, ((0, 0), (0, 0), (1, 1), (0, 0)))
    act_grad = flat_dot(backward_taps(grad_pad, row_count, col_count), spatial_back)
    act_grad = act_grad.reshape(inputs.shape)
    input_grad = (
        upstream.astype(jnp.float32) + silu_slope(inputs.astype(jnp.float32)) * act_grad
    ).astype(jnp.bfloat16)
    cell_count = (
        frame_count
        * lax.axis_size("tm")
        * row_count
        * lax.axis_size("height")
        * col_count
        * lax.axis_size("dp")
    )
    grad_scale = 1.0 / math.sqrt(cell_count)
    contract = (((0,), (0,)), ((), ()))
    local_taps = activ_taps.reshape(-1, 9 * channels)
    spatial_term = lax.dot_general(
        local_taps, frame_grad.reshape(-1, channels), contract, preferred_element_type=jnp.float32
    )
    temporal_term = lax.dot_general(
        frame_stack, upstream.reshape(-1, channels), contract, preferred_element_type=jnp.float32
    )
    weight_terms = jnp.concatenate([spatial_term, temporal_term], axis=0) * grad_scale
    summed = lax.psum(weight_terms, ("tm", "height", "dp")).astype(jnp.bfloat16)
    spatial_grad = summed[: 9 * channels].reshape(3, 3, channels, channels)
    temporal_grad = summed[9 * channels :].reshape(3, channels, channels)
    return (decoded[None], input_grad[None], spatial_grad, temporal_grad)


def solution(mesh):
    return jax.shard_map(
        local,
        mesh=mesh,
        in_specs=(
            P("dp", "tm", "height", None, None),
            P("dp", "tm", "height", None, None),
            P(),
            P(),
        ),
        out_specs=(
            P("dp", "tm", "height", None, None),
            P("dp", "tm", "height", None, None),
            P(),
            P(),
        ),
        check_vma=False,
    )
```

```python
import math

import jax
import jax.numpy as jnp
from jax import lax
from jax.sharding import PartitionSpec as P


def extended(x, sides, width):
    for axis, dim in sides:
        count, length = (lax.axis_size(axis), x.shape[dim])
        up = [(i, (i + 1) % count) for i in range(count - 1)]
        down = [(j, i) for i, j in up]
        last = lax.slice_in_dim(x, length - width, length, axis=dim)
        initial = lax.slice_in_dim(x, 0, width, axis=dim)
        before = lax.ppermute(last, axis, up)
        after = lax.ppermute(initial, axis, down)
        x = jnp.concatenate([before, x, after], axis=dim)
    return x


def from_behind(block, axis, distance):
    devices = range(lax.axis_size(axis))
    route = [(i - distance, i) for i in devices if i - distance in devices]
    return lax.ppermute(block, axis, route)


def silu_slope(values):
    sigmoid_value = jax.nn.sigmoid(values)
    return sigmoid_value * (1.0 + values * (1.0 - sigmoid_value))


def forward_taps(padded, row_count, col_count):
    pieces = [
        padded[:, row_tap : row_tap + row_count, col_tap : col_tap + col_count]
        for row_tap in range(3)
        for col_tap in range(3)
    ]
    return jnp.concatenate(pieces, axis=-1)


def backward_taps(padded, row_count, col_count):
    pieces = [
        padded[:, 2 - row_tap : 2 - row_tap + row_count, 2 - col_tap : 2 - col_tap + col_count]
        for row_tap in range(3)
        for col_tap in range(3)
    ]
    return jnp.concatenate(pieces, axis=-1)


def frame_taps(source, frame_count):
    return jnp.concatenate(
        [source[shift_tap : shift_tap + frame_count] for shift_tap in range(3)], axis=-1
    )


def flat_dot(left_side, right_side):
    return jnp.dot(
        left_side.reshape(-1, left_side.shape[-1]), right_side, preferred_element_type=jnp.float32
    )


def local(frames_in, cotangent, w_spatial, w_temporal):
    inputs = frames_in[0]
    upstream = cotangent[0]
    frame_count, row_count, col_count, channels = inputs.shape
    spatial_flat = w_spatial.reshape(9 * channels, channels)
    temporal_flat = w_temporal.reshape(3 * channels, channels)
    spatial_back = jnp.concatenate(
        [w_spatial[row_tap, col_tap].T for row_tap in range(3) for col_tap in range(3)], axis=0
    )
    temporal_back = jnp.concatenate([w_temporal[2].T, w_temporal[1].T, w_temporal[0].T], axis=0)
    first_shard = lax.axis_index("tm") == 0
    inputs_prev = from_behind(inputs[frame_count - 2 :], "tm", 1)
    upstream_next = from_behind(upstream[:2], "tm", -1)
    local_both = extended(jnp.concatenate([inputs, upstream], axis=-1), (("height", 1),), 1)
    rim_both = extended(
        jnp.concatenate([inputs_prev, upstream_next], axis=-1), (("height", 1),), 1
    )

    def spatial_forward(block):
        activ = jax.nn.silu(block.astype(jnp.float32)).astype(jnp.bfloat16)
        taps = forward_taps(jnp.pad(activ, ((0, 0), (0, 0), (1, 1), (0, 0))), row_count, col_count)
        out = flat_dot(taps, spatial_flat).astype(jnp.bfloat16)
        return taps, out.reshape(block.shape[0], row_count, col_count, channels)

    activ_taps, spatial_out = spatial_forward(local_both[..., :channels])
    unused, spatial_rim = spatial_forward(rim_both[..., :channels])
    repeated = jnp.broadcast_to(spatial_out[:1], (2,) + spatial_out.shape[1:])
    earlier = jnp.where(first_shard, repeated, spatial_rim)
    padded_frames = jnp.concatenate([earlier, spatial_out], axis=0)
    frame_stack = frame_taps(padded_frames, frame_count).reshape(-1, 3 * channels)
    temporal_out = jnp.dot(frame_stack, temporal_flat, preferred_element_type=jnp.float32).reshape(
        inputs.shape
    )
    decoded = (inputs.astype(jnp.float32) + temporal_out).astype(jnp.bfloat16)

    def frame_gradient(source):
        rows = source.shape[1]
        part = flat_dot(frame_taps(source, frame_count), temporal_back)
        first_up = source[0].reshape(-1, channels)
        second_up = source[1].reshape(-1, channels)
        fold = jnp.dot(first_up, w_temporal[0].T, preferred_element_type=jnp.float32)
        fold = fold + jnp.dot(first_up, w_temporal[1].T, preferred_element_type=jnp.float32)
        fold = fold + jnp.dot(second_up, w_temporal[0].T, preferred_element_type=jnp.float32)
        part = part.reshape(frame_count, rows * col_count, channels)
        part = part.at[0].add(jnp.where(first_shard, fold, 0.0))
        return part.astype(jnp.bfloat16).reshape(frame_count, rows, col_count, channels)

    frame_grad = frame_gradient(jnp.concatenate([upstream, upstream_next], axis=0))
    up_rows = jnp.concatenate([local_both[..., channels:], rim_both[..., channels:]], axis=0)
    edge_grad = frame_gradient(jnp.stack([up_rows[:, 0], up_rows[:, row_count + 1]], axis=1))
    frame_grad_full = jnp.concatenate([edge_grad[:, :1], frame_grad, edge_grad[:, 1:]], axis=1)
    grad_pad = jnp.pad(frame_grad_full, ((0, 0), (0, 0), (1, 1), (0, 0)))
    act_grad = flat_dot(backward_taps(grad_pad, row_count, col_count), spatial_back)
    act_grad = act_grad.reshape(inputs.shape)
    input_grad = (
        upstream.astype(jnp.float32) + silu_slope(inputs.astype(jnp.float32)) * act_grad
    ).astype(jnp.bfloat16)
    cell_count = (
        frame_count
        * lax.axis_size("tm")
        * row_count
        * lax.axis_size("height")
        * col_count
        * lax.axis_size("dp")
    )
    grad_scale = 1.0 / math.sqrt(cell_count)
    contract = (((0,), (0,)), ((), ()))
    local_taps = activ_taps.reshape(-1, 9 * channels)
    spatial_term = lax.dot_general(
        local_taps, frame_grad.reshape(-1, channels), contract, preferred_element_type=jnp.float32
    )
    temporal_term = lax.dot_general(
        frame_stack, upstream.reshape(-1, channels), contract, preferred_element_type=jnp.float32
    )
    spatial_sum, temporal_sum = lax.psum(
        (spatial_term * grad_scale, temporal_term * grad_scale), ("tm", "height", "dp")
    )
    spatial_grad = spatial_sum.astype(jnp.bfloat16).reshape(3, 3, channels, channels)
    temporal_grad = temporal_sum.astype(jnp.bfloat16).reshape(3, channels, channels)
    return (decoded[None], input_grad[None], spatial_grad, temporal_grad)


def solution(mesh):
    return jax.shard_map(
        local,
        mesh=mesh,
        in_specs=(
            P("dp", "tm", "height", None, None),
            P("dp", "tm", "height", None, None),
            P(),
            P(),
        ),
        out_specs=(
            P("dp", "tm", "height", None, None),
            P("dp", "tm", "height", None, None),
            P(),
            P(),
        ),
        check_vma=False,
    )
```

```python
import math

import jax
import jax.numpy as jnp
from jax import lax
from jax.sharding import PartitionSpec as P


def extended(x, sides, width):
    for axis, dim in sides:
        count, length = (lax.axis_size(axis), x.shape[dim])
        up = [(i, (i + 1) % count) for i in range(count - 1)]
        down = [(j, i) for i, j in up]
        last = lax.slice_in_dim(x, length - width, length, axis=dim)
        initial = lax.slice_in_dim(x, 0, width, axis=dim)
        before = lax.ppermute(last, axis, up)
        after = lax.ppermute(initial, axis, down)
        x = jnp.concatenate([before, x, after], axis=dim)
    return x


def from_behind(block, axis, distance):
    devices = range(lax.axis_size(axis))
    route = [(i - distance, i) for i in devices if i - distance in devices]
    return lax.ppermute(block, axis, route)


def silu_slope(values):
    sigmoid_value = jax.nn.sigmoid(values)
    return sigmoid_value * (1.0 + values * (1.0 - sigmoid_value))


def forward_taps(padded, row_count, col_count):
    pieces = [
        padded[:, row_tap : row_tap + row_count, col_tap : col_tap + col_count]
        for row_tap in range(3)
        for col_tap in range(3)
    ]
    return jnp.concatenate(pieces, axis=-1)


def backward_taps(padded, row_count, col_count):
    pieces = [
        padded[:, 2 - row_tap : 2 - row_tap + row_count, 2 - col_tap : 2 - col_tap + col_count]
        for row_tap in range(3)
        for col_tap in range(3)
    ]
    return jnp.concatenate(pieces, axis=-1)


def frame_taps(source, frame_count):
    return jnp.concatenate(
        [source[shift_tap : shift_tap + frame_count] for shift_tap in range(3)], axis=-1
    )


def flat_dot(left_side, right_side):
    return jnp.dot(
        left_side.reshape(-1, left_side.shape[-1]), right_side, preferred_element_type=jnp.float32
    )


def local(frames_in, cotangent, w_spatial, w_temporal):
    inputs = frames_in[0]
    upstream = cotangent[0]
    frame_count, row_count, col_count, channels = inputs.shape
    spatial_flat = w_spatial.reshape(9 * channels, channels)
    temporal_flat = w_temporal.reshape(3 * channels, channels)
    spatial_back = jnp.concatenate(
        [w_spatial[row_tap, col_tap].T for row_tap in range(3) for col_tap in range(3)], axis=0
    )
    temporal_back = jnp.concatenate([w_temporal[2].T, w_temporal[1].T, w_temporal[0].T], axis=0)
    first_shard = lax.axis_index("tm") == 0
    inputs_prev = from_behind(inputs, "tm", 1)[frame_count - 2 :]
    upstream_next = from_behind(upstream, "tm", -1)[:2]
    local_both = extended(jnp.concatenate([inputs, upstream], axis=-1), (("height", 1),), 1)
    rim_both = extended(
        jnp.concatenate([inputs_prev, upstream_next], axis=-1), (("height", 1),), 1
    )

    def spatial_forward(block):
        activ = jax.nn.silu(block.astype(jnp.float32)).astype(jnp.bfloat16)
        taps = forward_taps(jnp.pad(activ, ((0, 0), (0, 0), (1, 1), (0, 0))), row_count, col_count)
        out = flat_dot(taps, spatial_flat).astype(jnp.bfloat16)
        return taps, out.reshape(block.shape[0], row_count, col_count, channels)

    activ_taps, spatial_out = spatial_forward(local_both[..., :channels])
    unused, spatial_rim = spatial_forward(rim_both[..., :channels])
    repeated = jnp.broadcast_to(spatial_out[:1], (2,) + spatial_out.shape[1:])
    earlier = jnp.where(first_shard, repeated, spatial_rim)
    padded_frames = jnp.concatenate([earlier, spatial_out], axis=0)
    frame_stack = frame_taps(padded_frames, frame_count).reshape(-1, 3 * channels)
    temporal_out = jnp.dot(frame_stack, temporal_flat, preferred_element_type=jnp.float32).reshape(
        inputs.shape
    )
    decoded = (inputs.astype(jnp.float32) + temporal_out).astype(jnp.bfloat16)

    def frame_gradient(source):
        rows = source.shape[1]
        part = flat_dot(frame_taps(source, frame_count), temporal_back)
        first_up = source[0].reshape(-1, channels)
        second_up = source[1].reshape(-1, channels)
        fold = jnp.dot(first_up, w_temporal[0].T, preferred_element_type=jnp.float32)
        fold = fold + jnp.dot(first_up, w_temporal[1].T, preferred_element_type=jnp.float32)
        fold = fold + jnp.dot(second_up, w_temporal[0].T, preferred_element_type=jnp.float32)
        part = part.reshape(frame_count, rows * col_count, channels)
        part = part.at[0].add(jnp.where(first_shard, fold, 0.0))
        return part.astype(jnp.bfloat16).reshape(frame_count, rows, col_count, channels)

    frame_grad = frame_gradient(jnp.concatenate([upstream, upstream_next], axis=0))
    up_rows = jnp.concatenate([local_both[..., channels:], rim_both[..., channels:]], axis=0)
    edge_grad = frame_gradient(jnp.stack([up_rows[:, 0], up_rows[:, row_count + 1]], axis=1))
    frame_grad_full = jnp.concatenate([edge_grad[:, :1], frame_grad, edge_grad[:, 1:]], axis=1)
    grad_pad = jnp.pad(frame_grad_full, ((0, 0), (0, 0), (1, 1), (0, 0)))
    act_grad = flat_dot(backward_taps(grad_pad, row_count, col_count), spatial_back)
    act_grad = act_grad.reshape(inputs.shape)
    input_grad = (
        upstream.astype(jnp.float32) + silu_slope(inputs.astype(jnp.float32)) * act_grad
    ).astype(jnp.bfloat16)
    cell_count = (
        frame_count
        * lax.axis_size("tm")
        * row_count
        * lax.axis_size("height")
        * col_count
        * lax.axis_size("dp")
    )
    grad_scale = 1.0 / math.sqrt(cell_count)
    contract = (((0,), (0,)), ((), ()))
    local_taps = activ_taps.reshape(-1, 9 * channels)
    spatial_term = lax.dot_general(
        local_taps, frame_grad.reshape(-1, channels), contract, preferred_element_type=jnp.float32
    )
    temporal_term = lax.dot_general(
        frame_stack, upstream.reshape(-1, channels), contract, preferred_element_type=jnp.float32
    )
    spatial_sum, temporal_sum = lax.psum(
        (spatial_term * grad_scale, temporal_term * grad_scale), ("tm", "height", "dp")
    )
    spatial_grad = spatial_sum.astype(jnp.bfloat16).reshape(3, 3, channels, channels)
    temporal_grad = temporal_sum.astype(jnp.bfloat16).reshape(3, channels, channels)
    return (decoded[None], input_grad[None], spatial_grad, temporal_grad)


def solution(mesh):
    return jax.shard_map(
        local,
        mesh=mesh,
        in_specs=(
            P("dp", "tm", "height", None, None),
            P("dp", "tm", "height", None, None),
            P(),
            P(),
        ),
        out_specs=(
            P("dp", "tm", "height", None, None),
            P("dp", "tm", "height", None, None),
            P(),
            P(),
        ),
        check_vma=False,
    )
```
